32 devices in a mesh: stem: 8 (over y, x, core), grp: 4 (over z).
Axes of the slice: x: 2, y: 2, z: 4, core: 2. Of those that a mesh axis runs over, the one named last changes fastest.
Arguments:
- stem_tensor: float32 [32, 512, 512], P(None, 'stem', 'grp'), may hold values from -6 to 6
- left_factors: float32 [2, 16, 16, 256], P(None, 'grp'), may hold values from -0.375 to 0.375
- right_factors: float32 [2, 256, 1024], replicated, may hold values from -0.1875 to 0.1875
- index_labels: int32 [2, 9], replicated, may hold values from 0 to 8, each once within a row
Outputs:
- contracted: float32 [32, 512, 512], P(('stem', 'grp'))
The draws below stay inside these ranges and needn't reach their ends.
Inputs may be any that keep to these rules, and one draw needn't show every extreme that they name: `index_labels`: each row is a permutation of 0 to 8.
All inputs are finite; a program needn't handle non-finite values.
Results may differ from the reference program's by a relative error of at most 0.000098.
Values sent between devices are 32-bit elements; how exact they have to be, the bound alone decides.
No kernel may reach another device: no remote copies, remote signals or barrier semaphores. Data moves between devices by JAX's collectives and lax.ppermute only.
A program may use at most 64 MiB of HBM per device.

```python
import jax
import jax.numpy as jnp
from jax import lax

BITS = 9
BOND = 256
SHARED = 512
HALF = 16
LOW = 32
OPEN = 32


def shard_levels(stream_key, extent, cuts, low, high):
    factor_of = 1.0
    for axis_at, shards_of in cuts:
        heights = jax.random.uniform(jax.random.fold_in(jax.random.fold_in(stream_key, 6), axis_at), (shards_of,), jnp.float32, low / len(cuts), high / len(cuts))
        factor_of = factor_of * jnp.repeat(jnp.exp(heights), extent[axis_at] // shards_of).reshape((-1,) + (1,) * (len(extent) - 1 - axis_at))
    return factor_of


def noise(own_key, dims, width, bound, shards=(), kind=jnp.bfloat16):
    entries = width * jax.random.normal(own_key, dims, jnp.float32)
    if shards:
        entries = entries * shard_levels(own_key, dims, shards, -0.22, 0.18)
    return jnp.clip(entries, -bound, bound).astype(kind)


def setup_inputs(seed: int = 0) -> dict:
    seeds = jax.random.split(jax.random.key(seed), 5)
    stem_tensor = noise(seeds[0], (OPEN, SHARED, SHARED), 1.0, 6.0, ((1, 8), (2, 4)), jnp.float32)
    left_factors = noise(seeds[1], (2, HALF, HALF, BOND), BOND ** -0.5, 0.375, ((1, 4),), jnp.float32)
    right_factors = noise(seeds[2], (2, BOND, LOW * LOW), (LOW * LOW) ** -0.5, 0.1875, (), jnp.float32)
    index_labels = jax.vmap(lambda own: jax.random.permutation(own, BITS))(jax.random.split(seeds[3], 2)).reshape((2, BITS)).astype(jnp.int32)
    return dict(stem_tensor=stem_tensor, left_factors=left_factors, right_factors=right_factors, index_labels=index_labels)


def build_branch(left, right, bit_order):
    upper = left.shape[0]
    table = right.reshape(right.shape[0], LOW, LOW)
    product = jnp.einsum('abk,kcd->acbd', left, table, precision=lax.Precision.HIGHEST)
    whole_branch = product.reshape(upper * LOW, upper * LOW)
    row_ids = jnp.arange(upper * LOW, dtype=jnp.int32)
    source_rows = jnp.zeros_like(row_ids)
    for bit_number in range(bit_order.shape[0]):
        picked = jnp.bitwise_and(jnp.right_shift(row_ids, bit_number), 1)
        source_rows = source_rows + jnp.left_shift(picked, bit_order[bit_number].astype(jnp.int32))
    return jnp.take(whole_branch, source_rows, axis=0)


def reference(stem_tensor, left_factors, right_factors, index_labels):
    branch_one = build_branch(left_factors[0], right_factors[0], index_labels[0])
    branch_two = build_branch(left_factors[1], right_factors[1], index_labels[1])

    def contract_slab(stem_block):
        halfway = jnp.dot(stem_block, branch_one, precision=lax.Precision.HIGHEST)
        return jnp.dot(halfway.T, branch_two, precision=lax.Precision.HIGHEST)

    return lax.map(contract_slab, stem_tensor)
```

```python
import functools
import jax
import jax.numpy as jnp
from jax import lax
from jax.experimental import pallas as pl
from jax.experimental.pallas import tpu as pltpu
from jax.sharding import PartitionSpec as P


LOW = 32
LANES = 128


def split(x):
    high = x.astype(jnp.bfloat16)
    low = (x - high.astype(jnp.float32)).astype(jnp.bfloat16)
    return high, low


def dot3(a, b, dims):
    (a_high, a_low), (b_high, b_low) = a, b

    def one(x, y):
        return lax.dot_general(x, y, (dims, ((), ())), preferred_element_type=jnp.float32)

    return one(a_high, b_high) + (one(a_high, b_low) + one(a_low, b_high))


def branch_kernel(stems, grps, place, labels, pieces, right, *refs):
    outs, (ordered, product, wide) = refs[:-3], refs[-3:]
    branches, u_part, p_part, _ = pieces.shape[2:]
    upper_u, upper_p = stems * u_part, grps * p_part
    rows = upper_p * LOW
    cols = upper_u * LOW
    per_lane = LANES // LOW
    lane_group = lax.broadcasted_iota(jnp.int32, (upper_p, LANES), 1) // LOW
    row_id = lax.broadcasted_iota(jnp.int32, (rows, 1), 0)
    col_id = lax.broadcasted_iota(jnp.int32, (rows, rows), 1)
    for b in range(branches):
        for s in range(stems):
            for g in range(grps):
                block = pieces[place[0] ^ s, place[1] ^ g, b]
                for u in range(u_part):
                    ordered[pl.ds((s * u_part + u) * upper_p + g * p_part, p_part), :] = block[u]
        product[...] = dot3(split(ordered[...]), split(right[b]), ((1,), (0,)))
        for c in range(LOW * LOW // LANES):
            for a in range(cols // LANES):
                tiles = [
                    product[pl.ds((a * per_lane + k) * upper_p, upper_p), pl.ds(c * LANES, LANES)]
                    for k in range(per_lane)
                ]
                for j in range(per_lane):
                    merged = None
                    for k in range(per_lane):
                        moved = pltpu.roll(tiles[k], ((k - j) * LOW) % LANES, 1) if k != j else tiles[k]
                        merged = moved if merged is None else jnp.where(lane_group == k, moved, merged)
                    wide[pl.ds((c * per_lane + j) * upper_p, upper_p), pl.ds(a * LANES, LANES)] = merged
        source = jnp.zeros_like(row_id)
        for j in range(labels.shape[1]):
            source = source + jnp.left_shift(jnp.bitwise_and(jnp.right_shift(row_id, j), 1), labels[b, j])
        source = jnp.bitwise_and(source, LOW - 1) * upper_p + jnp.right_shift(source, LOW.bit_length() - 1)
        chosen = (col_id == source).astype(jnp.float32).astype(jnp.bfloat16)
        for out, part in zip(outs[2 * b : 2 * b + 2], split(wide[...])):
            picked = jnp.dot(chosen, part, preferred_element_type=jnp.float32)
            out[...] = (picked.T if b == 0 else picked).astype(jnp.bfloat16)


def make_branches(pieces, right, labels, place):
    stems, grps, _, u_part, p_part, bond = pieces.shape
    upper_u, upper_p = stems * u_part, grps * p_part
    rows, cols = upper_p * LOW, upper_u * LOW
    out = jax.ShapeDtypeStruct((rows, cols), jnp.bfloat16)
    return pl.pallas_call(
        functools.partial(branch_kernel, stems, grps),
        out_shape=[jax.ShapeDtypeStruct((cols, rows), jnp.bfloat16)] * 2 + [out] * 2,
        in_specs=[pl.BlockSpec(memory_space=pltpu.SMEM)] * 2 + [pl.BlockSpec(memory_space=pltpu.VMEM)] * 2,
        out_specs=[pl.BlockSpec(memory_space=pltpu.VMEM)] * 4,
        scratch_shapes=[
            pltpu.VMEM((upper_u * upper_p, bond), jnp.float32),
            pltpu.VMEM((upper_u * upper_p, right.shape[2]), jnp.float32),
            pltpu.VMEM((rows, cols), jnp.float32),
        ],
        name="branches",
    )(place, labels, pieces, right)


def stem_kernel(stems, grps, blocks, one_high, one_low, two_high, two_low, out):
    inner = blocks.shape[2]
    x = blocks[...].reshape(stems, grps, blocks.shape[1], inner)
    slab = jnp.concatenate([x[:, g].reshape(-1, inner) for g in range(grps)], axis=1)
    turned = dot3((one_high[...], one_low[...]), split(slab), ((1,), (1,)))
    out[...] = dot3(split(turned), (two_high[...], two_low[...]), ((1,), (0,)))


def contract(blocks, parts, stems, grps):
    if blocks.shape[2] % LANES:
        x = blocks.reshape(stems, grps, *blocks.shape[1:])
        blocks = x.transpose(0, 2, 1, 3).reshape(stems, blocks.shape[1], -1)
        grps = 1
    shape = (parts[0].shape[0], parts[2].shape[1])
    return pl.pallas_call(
        functools.partial(stem_kernel, stems, grps),
        out_shape=jax.ShapeDtypeStruct(shape, jnp.float32),
        in_specs=[pl.BlockSpec(memory_space=pltpu.VMEM)] * 5,
        out_specs=pl.BlockSpec(memory_space=pltpu.VMEM),
        name="contract",
    )(blocks, *parts)


def on_device(stem_tensor, left_factors, right_factors, index_labels):
    stems, grps = lax.axis_size("stem"), lax.axis_size("grp")
    s, g = lax.axis_index("stem"), lax.axis_index("grp")
    branches, p_part, upper, bond = left_factors.shape
    u_part = upper // stems
    own = lax.dynamic_slice_in_dim(left_factors, s * u_part, u_part, axis=2)
    own = own.transpose(0, 2, 1, 3).reshape(-1, bond)
    near = [own] + [lax.ppermute(own, "grp", [(j, j ^ k) for j in range(grps)]) for k in range(1, grps)]
    blocks = lax.all_to_all(stem_tensor, ("stem", "grp"), split_axis=0, concat_axis=0, tiled=True)
    column = jnp.concatenate(near, axis=0)
    plane = [column] + [lax.ppermute(column, "stem", [(j, j ^ k) for j in range(stems)]) for k in range(2, stems, 2)]
    half = jnp.stack(plane)
    other = lax.ppermute(half, "stem", [(j, j ^ 1) for j in range(stems)])
    pieces = jnp.stack([half, other], axis=1).reshape(stems, grps, branches, u_part, p_part, bond)
    place = jnp.stack([s, g]).astype(jnp.int32)
    parts = make_branches(pieces, right_factors, index_labels, place)
    count = stem_tensor.shape[0] // (stems * grps)
    blocks = blocks.reshape(stems * grps, count, *stem_tensor.shape[1:])
    return jnp.stack([contract(blocks[:, o], parts, stems, grps) for o in range(count)])


def solution(mesh):
    placed = (P(None, "stem", "grp"), P(None, "grp", None, None), P(), P())
    return jax.shard_map(
        on_device,
        mesh=mesh,
        in_specs=placed,
        out_specs=P(("stem", "grp"), None, None),
        check_vma=False,
    )
```

```python
import functools
import jax
import jax.numpy as jnp
from jax import lax
from jax.experimental import pallas as pl
from jax.experimental.pallas import tpu as pltpu
from jax.sharding import PartitionSpec as P


LOW = 32
LANES = 128
LIMIT = 20 * 2**20
VMEM = pl.BlockSpec(memory_space=pltpu.VMEM)
AWAY = pl.BlockSpec(memory_space=pl.ANY)
SMEM = pl.BlockSpec(memory_space=pltpu.SMEM)


def on_chip(x):
    return pltpu.with_memory_space_constraint(x, pltpu.VMEM)


def off_chip(x):
    return pltpu.with_memory_space_constraint(x, pltpu.HBM)


def split(x):
    high = x.astype(jnp.bfloat16)
    low = (x - high.astype(jnp.float32)).astype(jnp.bfloat16)
    return high, low


def dot3(a, b, dims):
    (a_high, a_low), (b_high, b_low) = a, b

    def one(x, y):
        return lax.dot_general(x, y, (dims, ((), ())), preferred_element_type=jnp.float32)

    return one(a_high, b_high) + (one(a_high, b_low) + one(a_low, b_high))


def order_rows(place, own, near, same, other, ordered, b):
    _, p_part, upper, _ = own.shape
    chips = same.shape[0]
    core, chip = jnp.bitwise_and(place[0], 1), jnp.right_shift(place[0], 1)
    far = upper // chips
    per_u = 4 * p_part
    for n, ref in enumerate((own, near)):
        for p in range(p_part):
            rows = ref[b, p]
            for u in range(upper):
                ordered[pl.ds(u * per_u + n * p_part + p, 1), :] = rows[u : u + 1]
    for c in range(chips):
        for e in range(2):
            fetched = jnp.where(core == e, same[chip ^ c], other[chip ^ c])
            for u in range(far):
                at = (c * far + u) * per_u + (2 + e) * p_part
                ordered[pl.ds(at, p_part), :] = fetched[(b * far + u) * p_part :][:p_part]


def branch_kernel(fetched, place, labels, *refs):
    ordered_refs, refs = refs[: 4 if fetched else 1], refs[4 if fetched else 1 :]
    right_away, one_high, one_low, two, ordered, product, wide, right, arrived = refs
    brings = [pltpu.make_async_copy(right_away.at[b], right.at[b], arrived.at[b]) for b in range(right.shape[0])]
    for bring in brings:
        bring.start()
    branches = right.shape[0]
    rows, cols = wide.shape
    upper_p = rows // LOW
    per_lane = LANES // LOW
    lane_group = lax.broadcasted_iota(jnp.int32, (upper_p, LANES), 1) // LOW
    row_id = lax.broadcasted_iota(jnp.int32, (rows, 1), 0)
    col_id = lax.broadcasted_iota(jnp.int32, (rows, rows), 1)
    for b in range(branches):
        if fetched:
            order_rows(place, *ordered_refs, ordered, b)
        else:
            ordered[...] = ordered_refs[0][b]
        brings[b].wait()
        product[...] = dot3(split(ordered[...]), split(right[b]), ((1,), (0,)))
        for c in range(LOW * LOW // LANES):
            for a in range(cols // LANES):
                tiles = [
                    product[pl.ds((a * per_lane + k) * upper_p, upper_p), pl.ds(c * LANES, LANES)]
                    for k in range(per_lane)
                ]
                for j in range(per_lane):
                    merged = None
                    for k in range(per_lane):
                        moved = pltpu.roll(tiles[k], ((k - j) * LOW) % LANES, 1) if k != j else tiles[k]
                        merged = moved if merged is None else jnp.where(lane_group == k, moved, merged)
                    wide[pl.ds((c * per_lane + j) * upper_p, upper_p), pl.ds(a * LANES, LANES)] = merged
        source = jnp.zeros_like(row_id)
        for j in range(labels.shape[1]):
            source = source + jnp.left_shift(jnp.bitwise_and(jnp.right_shift(row_id, j), 1), labels[b, j])
        upper = jnp.bitwise_xor(jnp.right_shift(source, LOW.bit_length() - 1), place[1])
        source = jnp.bitwise_and(source, LOW - 1) * upper_p + upper
        chosen = (col_id == source).astype(jnp.float32).astype(jnp.bfloat16)
        for n, part in enumerate(split(wide[...])):
            picked = jnp.dot(chosen, part, preferred_element_type=jnp.float32)
            if b == 0:
                (one_high, one_low)[n][...] = picked.T.astype(jnp.bfloat16)
            else:
                two[n] = picked.astype(jnp.bfloat16)


def make_branches(firsts, right, labels, place, rows, cols):
    branches, bond, low_pairs = right.shape
    fetched = len(firsts) > 1
    return pl.pallas_call(
        functools.partial(branch_kernel, fetched),
        out_shape=[pltpu.VMEM((cols, rows), jnp.bfloat16)] * 2 + [pltpu.HBM((2, rows, cols), jnp.bfloat16)],
        in_specs=[SMEM, SMEM] + [VMEM] * len(firsts) + [AWAY],
        out_specs=[VMEM] * 3,
        scratch_shapes=[
            pltpu.VMEM((rows * cols // (LOW * LOW), bond), jnp.float32),
            pltpu.VMEM((rows * cols // (LOW * LOW), low_pairs), jnp.float32),
            pltpu.VMEM((rows, cols), jnp.float32),
            pltpu.VMEM(right.shape, right.dtype),
            pltpu.SemaphoreType.DMA((branches,)),
        ],
        compiler_params=pltpu.CompilerParams(vmem_limit_bytes=LIMIT),
        name="branches",
    )(place, labels, *(on_chip(x) for x in firsts), off_chip(right))


def stem_kernel(stems, grps, steps, blocks, one_high, one_low, two_away, out_away, two, out, arrived, left):
    bring = pltpu.make_async_copy(two_away, two, arrived)
    bring.start()
    inner = blocks.shape[2]
    x = blocks[...].reshape(stems, grps, blocks.shape[1], inner)
    slab = jnp.concatenate([x[:, g].reshape(-1, inner) for g in range(grps)], axis=1)
    turned = split(dot3((one_high[...], one_low[...]), split(slab), ((1,), (1,))))
    bring.wait()
    sends, start = [], 0
    for n, size in enumerate(steps):
        rows = pl.ds(start, size)
        out[rows, :] = dot3(
            tuple(t[start : start + size] for t in turned), (two[0], two[1]), ((1,), (0,))
        )
        sends.append(pltpu.make_async_copy(out.at[rows], out_away.at[rows], left.at[n]))
        sends[-1].start()
        start += size
    for send in sends:
        send.wait()


def contract(blocks, parts, stems, grps):
    if blocks.shape[2] % LANES:
        x = blocks.reshape(stems, grps, *blocks.shape[1:])
        blocks = x.transpose(0, 2, 1, 3).reshape(stems, blocks.shape[1], -1)
        grps = 1
    one_high, one_low, two = parts
    shape = (one_high.shape[0], two.shape[2])
    steps = (shape[0] // 2, shape[0] // 4, shape[0] // 4)
    return pl.pallas_call(
        functools.partial(stem_kernel, stems, grps, steps),
        out_shape=jax.ShapeDtypeStruct(shape, jnp.float32),
        in_specs=[VMEM] * 3 + [AWAY],
        out_specs=AWAY,
        scratch_shapes=[
            pltpu.VMEM(two.shape, two.dtype),
            pltpu.VMEM(shape, jnp.float32),
            pltpu.SemaphoreType.DMA,
            pltpu.SemaphoreType.DMA((len(steps),)),
        ],
        compiler_params=pltpu.CompilerParams(vmem_limit_bytes=LIMIT),
        name="contract",
    )(on_chip(blocks), on_chip(one_high), on_chip(one_low), off_chip(two))


def fetch(left, stems, grps, s):
    _, _, upper, bond = left.shape
    far = 2 * upper // stems
    near = lax.ppermute(left, "grp", [(j, j ^ 1) for j in range(grps)])
    part = lax.dynamic_slice_in_dim(left, (s // 2) * far, far, axis=2).transpose(0, 2, 1, 3).reshape(-1, bond)
    pairs = [(i * grps + j, i * grps + (j ^ (2 + i % 2))) for i in range(stems) for j in range(grps)]
    column = lax.ppermute(part, ("stem", "grp"), pairs)
    plane = [column] + [lax.ppermute(column, "stem", [(j, j ^ k) for j in range(stems)]) for k in range(2, stems, 2)]
    same = jnp.stack(plane)
    other = lax.ppermute(same, "stem", [(j, j ^ 1) for j in range(stems)])
    return left, near, same, other


def on_device(stem_tensor, left_factors, right_factors, index_labels):
    stems, grps = lax.axis_size("stem"), lax.axis_size("grp")
    s, g = lax.axis_index("stem"), lax.axis_index("grp")
    branches, p_part, upper, bond = left_factors.shape
    rows, cols = p_part * grps * LOW, upper * LOW
    if grps == 4:
        firsts, cross = fetch(left_factors, stems, grps, s), g * p_part
    else:
        whole = lax.all_gather(left_factors, "grp", axis=1, tiled=True)
        firsts, cross = (whole.transpose(0, 2, 1, 3).reshape(branches, -1, bond),), 0 * g
    blocks = lax.all_to_all(stem_tensor, ("stem", "grp"), split_axis=0, concat_axis=0, tiled=True)
    place = jnp.stack([s, cross]).astype(jnp.int32)
    parts = make_branches(firsts, right_factors, index_labels, place, rows, cols)
    count = stem_tensor.shape[0] // (stems * grps)
    blocks = blocks.reshape(stems * grps, count, *stem_tensor.shape[1:])
    return jnp.stack([contract(blocks[:, o], parts, stems, grps) for o in range(count)])


def solution(mesh):
    placed = (P(None, "stem", "grp"), P(None, "grp", None, None), P(), P())
    return jax.shard_map(
        on_device,
        mesh=mesh,
        in_specs=placed,
        out_specs=P(("stem", "grp"), None, None),
        check_vma=False,
    )
```

```python
import functools
import jax
import jax.numpy as jnp
from jax import lax
from jax.experimental import pallas as pl
from jax.experimental.pallas import tpu as pltpu
from jax.sharding import PartitionSpec as P


LOW = 32
LANES = 128
LIMIT = 20 * 2**20
VMEM = pl.BlockSpec(memory_space=pltpu.VMEM)
AWAY = pl.BlockSpec(memory_space=pl.ANY)
SMEM = pl.BlockSpec(memory_space=pltpu.SMEM)


def on_chip(x):
    return pltpu.with_memory_space_constraint(x, pltpu.VMEM)


def off_chip(x):
    return pltpu.with_memory_space_constraint(x, pltpu.HBM)


def split(x):
    high = x.astype(jnp.bfloat16)
    low = (x - high.astype(jnp.float32)).astype(jnp.bfloat16)
    return high, low


def dot3(a, b, dims):
    (a_high, a_low), (b_high, b_low) = a, b

    def one(x, y):
        return lax.dot_general(x, y, (dims, ((), ())), preferred_element_type=jnp.float32)

    return one(a_high, b_high) + (one(a_high, b_low) + one(a_low, b_high))


def order_rows(place, own, near, same, other, ordered, b):
    _, p_part, upper, _ = own.shape
    core = jnp.bitwise_and(place[0], 1)
    per_u = 4 * p_part
    for p in range(p_part):
        mine, its = same[b, p], other[b, p]
        for n, rows in enumerate((own[b, p], near[b, p], jnp.where(core == 0, mine, its), jnp.where(core == 0, its, mine))):
            for u in range(upper):
                ordered[pl.ds(u * per_u + n * p_part + p, 1), :] = rows[u : u + 1]


def regroup(tiles, lane_group):
    for bit in range(len(tiles).bit_length() - 1):
        step, shift = 1 << bit, LOW << bit
        upper = jnp.bitwise_and(jnp.right_shift(lane_group, bit), 1) == 1
        for k in range(len(tiles)):
            if k & step == 0:
                low, high = tiles[k], tiles[k | step]
                tiles[k] = jnp.where(upper, pltpu.roll(high, shift, 1), low)
                tiles[k | step] = jnp.where(upper, high, pltpu.roll(low, LANES - shift, 1))
    return tiles


def branch_kernel(fetched, place, labels, *refs):
    count = 4 if fetched else 1
    away, refs = refs[:count], refs[count:]
    right_away, one_high, one_low, two, ordered, product, wide, chosen, right, arrived = refs[:10]
    near_by, here = refs[10:-1], refs[-1]
    brings = [pltpu.make_async_copy(right_away.at[b], right.at[b], arrived.at[b]) for b in range(right.shape[0])]
    takes = [pltpu.make_async_copy(x, y, here.at[n]) for n, (x, y) in enumerate(zip(away, near_by))]
    for take in takes:
        take.start()
    brings[0].start()
    branches = right.shape[0]
    rows, cols = wide.shape
    upper_p = rows // LOW
    per_lane = LANES // LOW
    lane_group = lax.broadcasted_iota(jnp.int32, (upper_p, LANES), 1) // LOW
    to_id = lax.broadcasted_iota(jnp.int32, (1, rows), 1)
    from_id = lax.broadcasted_iota(jnp.int32, (rows, rows), 0)
    for b in range(branches):
        source = jnp.zeros_like(to_id)
        for j in range(labels.shape[1]):
            source = source + jnp.left_shift(jnp.bitwise_and(jnp.right_shift(to_id, j), 1), labels[b, j])
        upper = jnp.bitwise_xor(jnp.right_shift(source, LOW.bit_length() - 1), place[1])
        source = jnp.bitwise_and(source, LOW - 1) * upper_p + upper
        chosen[b] = (from_id == source).astype(jnp.float32).astype(jnp.bfloat16)
    for take in takes:
        take.wait()
    for b in range(branches):
        if fetched:
            order_rows(place, *near_by, ordered, b)
        else:
            ordered[...] = near_by[0][b]
        brings[b].wait()
        if b + 1 < branches:
            brings[b + 1].start()
        product[...] = dot3(split(ordered[...]), split(right[b]), ((1,), (0,)))
        for c in range(LOW * LOW // LANES):
            for a in range(cols // LANES):
                tiles = [
                    product[pl.ds((a * per_lane + k) * upper_p, upper_p), pl.ds(c * LANES, LANES)]
                    for k in range(per_lane)
                ]
                for j, tile in enumerate(regroup(tiles, lane_group)):
                    wide[pl.ds((c * per_lane + j) * upper_p, upper_p), pl.ds(a * LANES, LANES)] = tile
        for n, part in enumerate(split(wide[...])):
            sides = (part, chosen[b]) if b == 0 else (chosen[b], part)
            picked = lax.dot_general(*sides, (((0,), (0,)), ((), ())), preferred_element_type=jnp.float32)
            if b == 0:
                (one_high, one_low)[n][...] = picked.astype(jnp.bfloat16)
            else:
                two[n] = picked.astype(jnp.bfloat16)


def make_branches(firsts, right, labels, place, rows, cols):
    branches, bond, low_pairs = right.shape
    fetched = len(firsts) > 1
    return pl.pallas_call(
        functools.partial(branch_kernel, fetched),
        out_shape=[pltpu.VMEM((cols, rows), jnp.bfloat16)] * 2 + [pltpu.VMEM((2, rows, cols), jnp.bfloat16)],
        in_specs=[SMEM, SMEM] + [AWAY] * (len(firsts) + 1),
        out_specs=[VMEM] * 3,
        scratch_shapes=[
            pltpu.VMEM((rows * cols // (LOW * LOW), bond), jnp.float32),
            pltpu.VMEM((rows * cols // (LOW * LOW), low_pairs), jnp.float32),
            pltpu.VMEM((rows, cols), jnp.float32),
            pltpu.VMEM((branches, rows, rows), jnp.bfloat16),
            pltpu.VMEM(right.shape, right.dtype),
            pltpu.SemaphoreType.DMA((branches,)),
            *(pltpu.VMEM(x.shape, x.dtype) for x in firsts),
            pltpu.SemaphoreType.DMA((len(firsts),)),
        ],
        compiler_params=pltpu.CompilerParams(vmem_limit_bytes=LIMIT),
        name="branches",
    )(place, labels, *(off_chip(x) for x in firsts), off_chip(right))


def stem_kernel(stems, grps, steps, blocks, one_high, one_low, two, out_away, out, left):
    inner = blocks.shape[2]
    x = blocks[...].reshape(stems, grps, blocks.shape[1], inner)
    slab = jnp.concatenate([x[:, g].reshape(-1, inner) for g in range(grps)], axis=1)
    turned = split(dot3((one_high[...], one_low[...]), split(slab), ((1,), (1,))))
    sends, start = [], 0
    for n, size in enumerate(steps):
        rows = pl.ds(start, size)
        out[rows, :] = dot3(
            tuple(t[start : start + size] for t in turned), (two[0], two[1]), ((1,), (0,))
        )
        sends.append(pltpu.make_async_copy(out.at[rows], out_away.at[rows], left.at[n]))
        sends[-1].start()
        start += size
    for send in sends:
        send.wait()


def contract(blocks, parts, stems, grps):
    if blocks.shape[2] % LANES:
        x = blocks.reshape(stems, grps, *blocks.shape[1:])
        blocks = x.transpose(0, 2, 1, 3).reshape(stems, blocks.shape[1], -1)
        grps = 1
    one_high, one_low, two = parts
    shape = (one_high.shape[0], two.shape[2])
    steps = (shape[0] // 2, shape[0] // 4, shape[0] // 4)
    return pl.pallas_call(
        functools.partial(stem_kernel, stems, grps, steps),
        out_shape=jax.ShapeDtypeStruct(shape, jnp.float32),
        in_specs=[VMEM] * 4,
        out_specs=AWAY,
        scratch_shapes=[
            pltpu.VMEM(shape, jnp.float32),
            pltpu.SemaphoreType.DMA((len(steps),)),
        ],
        compiler_params=pltpu.CompilerParams(vmem_limit_bytes=LIMIT),
        name="contract",
    )(on_chip(blocks), on_chip(one_high), on_chip(one_low), on_chip(two))


def fetch(left, stems, grps):
    near = lax.ppermute(left, "grp", [(j, j ^ 1) for j in range(grps)])
    pairs = [(i * grps + j, i * grps + (j ^ (2 + i % 2))) for i in range(stems) for j in range(grps)]
    same = lax.ppermute(left, ("stem", "grp"), pairs)
    other = lax.ppermute(same, "stem", [(j, j ^ 1) for j in range(stems)])
    return left, near, same, other


def on_device(stem_tensor, left_factors, right_factors, index_labels):
    stems, grps = lax.axis_size("stem"), lax.axis_size("grp")
    s, g = lax.axis_index("stem"), lax.axis_index("grp")
    branches, p_part, upper, bond = left_factors.shape
    rows, cols = p_part * grps * LOW, upper * LOW
    if (stems % 2, grps) == (0, 4):
        firsts, cross = fetch(left_factors, stems, grps), g * p_part
    else:
        whole = lax.all_gather(left_factors, "grp", axis=1, tiled=True)
        firsts, cross = (whole.transpose(0, 2, 1, 3).reshape(branches, -1, bond),), 0 * g
    blocks = lax.all_to_all(stem_tensor, ("stem", "grp"), split_axis=0, concat_axis=0, tiled=True)
    place = jnp.stack([s, cross]).astype(jnp.int32)
    parts = make_branches(firsts, right_factors, index_labels, place, rows, cols)
    count = stem_tensor.shape[0] // (stems * grps)
    blocks = blocks.reshape(stems * grps, count, *stem_tensor.shape[1:])
    return jnp.stack([contract(blocks[:, o], parts, stems, grps) for o in range(count)])


def solution(mesh):
    placed = (P(None, "stem", "grp"), P(None, "grp", None, None), P(), P())
    return jax.shard_map(
        on_device,
        mesh=mesh,
        in_specs=placed,
        out_specs=P(("stem", "grp"), None, None),
        check_vma=False,
    )
```

```python
import functools
import jax
import jax.numpy as jnp
from jax import lax
from jax.experimental import pallas as pl
from jax.experimental.pallas import tpu as pltpu
from jax.sharding import PartitionSpec as P


LOW = 32
LANES = 128
LIMIT = 20 * 2**20
VMEM = pl.BlockSpec(memory_space=pltpu.VMEM)
AWAY = pl.BlockSpec(memory_space=pl.ANY)
SMEM = pl.BlockSpec(memory_space=pltpu.SMEM)


def on_chip(x):
    return pltpu.with_memory_space_constraint(x, pltpu.VMEM)


def off_chip(x):
    return pltpu.with_memory_space_constraint(x, pltpu.HBM)


def split(x):
    high = x.astype(jnp.bfloat16)
    low = (x - high.astype(jnp.float32)).astype(jnp.bfloat16)
    return high, low


def dot3(a, b, dims):
    (a_high, a_low), (b_high, b_low) = a, b

    def one(x, y):
        return lax.dot_general(x, y, (dims, ((), ())), preferred_element_type=jnp.float32)

    return one(a_high, b_high) + (one(a_high, b_low) + one(a_low, b_high))


def order_rows(place, own, first, swapped, second, passed, ordered, b):
    _, p_part, upper, _ = own.shape
    core = jnp.bitwise_and(place[0], 1)
    per_u = 4 * p_part
    for p in range(p_part):
        mine, its = first[b, p], swapped[b, p]
        slots = (
            own[b, p],
            jnp.where(core == 1, mine, its),
            jnp.where(core == 1, its, mine),
            jnp.where(core == 1, passed[b, p], second[b, p]),
        )
        for n, rows in enumerate(slots):
            for u in range(upper):
                ordered[pl.ds(u * per_u + n * p_part + p, 1), :] = rows[u : u + 1]


def regroup(tiles, lane_group):
    for bit in range(len(tiles).bit_length() - 1):
        step, shift = 1 << bit, LOW << bit
        upper = jnp.bitwise_and(jnp.right_shift(lane_group, bit), 1) == 1
        for k in range(len(tiles)):
            if k & step == 0:
                low, high = tiles[k], tiles[k | step]
                tiles[k] = jnp.where(upper, pltpu.roll(high, shift, 1), low)
                tiles[k | step] = jnp.where(upper, high, pltpu.roll(low, LANES - shift, 1))
    return tiles


def branch_kernel(fetched, place, labels, *refs):
    count = 5 if fetched else 1
    away, refs = refs[:count], refs[count:]
    right_away, one_high, one_low, two, ordered, product, wide, chosen, right, arrived = refs[:10]
    near_by, here = refs[10:-1], refs[-1]
    brings = [pltpu.make_async_copy(right_away.at[b], right.at[b], arrived.at[b]) for b in range(right.shape[0])]
    takes = [pltpu.make_async_copy(x, y, here.at[n]) for n, (x, y) in enumerate(zip(away, near_by))]
    for take in takes:
        take.start()
    brings[0].start()
    branches = right.shape[0]
    rows, cols = wide.shape
    upper_p = rows // LOW
    per_lane = LANES // LOW
    lane_group = lax.broadcasted_iota(jnp.int32, (upper_p, LANES), 1) // LOW
    to_id = lax.broadcasted_iota(jnp.int32, (1, rows), 1)
    from_id = lax.broadcasted_iota(jnp.int32, (rows, rows), 0)
    for b in range(branches):
        source = jnp.zeros_like(to_id)
        for j in range(labels.shape[1]):
            source = source + jnp.left_shift(jnp.bitwise_and(jnp.right_shift(to_id, j), 1), labels[b, j])
        upper = jnp.bitwise_xor(jnp.right_shift(source, LOW.bit_length() - 1), place[1])
        upper = jnp.where(upper >= upper_p // 2, jnp.bitwise_xor(upper, place[2]), upper)
        source = jnp.bitwise_and(source, LOW - 1) * upper_p + upper
        chosen[b] = (from_id == source).astype(jnp.float32).astype(jnp.bfloat16)
    for take in takes:
        take.wait()
    for b in range(branches):
        if fetched:
            order_rows(place, *near_by, ordered, b)
        else:
            ordered[...] = near_by[0][b]
        brings[b].wait()
        if b + 1 < branches:
            brings[b + 1].start()
        product[...] = dot3(split(ordered[...]), split(right[b]), ((1,), (0,)))
        for c in range(LOW * LOW // LANES):
            for a in range(cols // LANES):
                tiles = [
                    product[pl.ds((a * per_lane + k) * upper_p, upper_p), pl.ds(c * LANES, LANES)]
                    for k in range(per_lane)
                ]
                for j, tile in enumerate(regroup(tiles, lane_group)):
                    wide[pl.ds((c * per_lane + j) * upper_p, upper_p), pl.ds(a * LANES, LANES)] = tile
        for n, part in enumerate(split(wide[...])):
            sides = (part, chosen[b]) if b == 0 else (chosen[b], part)
            picked = lax.dot_general(*sides, (((0,), (0,)), ((), ())), preferred_element_type=jnp.float32)
            if b == 0:
                (one_high, one_low)[n][...] = picked.astype(jnp.bfloat16)
            else:
                two[n] = picked.astype(jnp.bfloat16)


def make_branches(firsts, right, labels, place, rows, cols):
    branches, bond, low_pairs = right.shape
    fetched = len(firsts) > 1
    return pl.pallas_call(
        functools.partial(branch_kernel, fetched),
        out_shape=[pltpu.VMEM((cols, rows), jnp.bfloat16)] * 2 + [pltpu.VMEM((2, rows, cols), jnp.bfloat16)],
        in_specs=[SMEM, SMEM] + [AWAY] * (len(firsts) + 1),
        out_specs=[VMEM] * 3,
        scratch_shapes=[
            pltpu.VMEM((rows * cols // (LOW * LOW), bond), jnp.float32),
            pltpu.VMEM((rows * cols // (LOW * LOW), low_pairs), jnp.float32),
            pltpu.VMEM((rows, cols), jnp.float32),
            pltpu.VMEM((branches, rows, rows), jnp.bfloat16),
            pltpu.VMEM(right.shape, right.dtype),
            pltpu.SemaphoreType.DMA((branches,)),
            *(pltpu.VMEM(x.shape, x.dtype) for x in firsts),
            pltpu.SemaphoreType.DMA((len(firsts),)),
        ],
        compiler_params=pltpu.CompilerParams(vmem_limit_bytes=LIMIT),
        name="branches",
    )(place, labels, *(off_chip(x) for x in firsts), off_chip(right))


def stem_kernel(stems, grps, steps, blocks, one_high, one_low, two, out_away, out, left):
    inner = blocks.shape[2]
    x = blocks[...].reshape(stems, grps, blocks.shape[1], inner)
    slab = jnp.concatenate([x[:, g].reshape(-1, inner) for g in range(grps)], axis=1)
    turned = split(dot3((one_high[...], one_low[...]), split(slab), ((1,), (1,))))
    sends, start = [], 0
    for n, size in enumerate(steps):
        rows = pl.ds(start, size)
        out[rows, :] = dot3(
            tuple(t[start : start + size] for t in turned), (two[0], two[1]), ((1,), (0,))
        )
        sends.append(pltpu.make_async_copy(out.at[rows], out_away.at[rows], left.at[n]))
        sends[-1].start()
        start += size
    for send in sends:
        send.wait()


def contract(blocks, parts, stems, grps):
    if blocks.shape[2] % LANES:
        x = blocks.reshape(stems, grps, *blocks.shape[1:])
        blocks = x.transpose(0, 2, 1, 3).reshape(stems, blocks.shape[1], -1)
        grps = 1
    one_high, one_low, two = parts
    shape = (one_high.shape[0], two.shape[2])
    steps = (shape[0] * 3 // 4, shape[0] // 4)
    return pl.pallas_call(
        functools.partial(stem_kernel, stems, grps, steps),
        out_shape=jax.ShapeDtypeStruct(shape, jnp.float32),
        in_specs=[VMEM] * 4,
        out_specs=AWAY,
        scratch_shapes=[
            pltpu.VMEM(shape, jnp.float32),
            pltpu.SemaphoreType.DMA((len(steps),)),
        ],
        compiler_params=pltpu.CompilerParams(vmem_limit_bytes=LIMIT),
        name="contract",
    )(on_chip(blocks), on_chip(one_high), on_chip(one_low), on_chip(two))


def fetch(left, stems, grps):
    offsets = [1 if i % 2 else 2 + i // 2 % 2 for i in range(stems)]
    pairs = [(i * grps + j, i * grps + (j ^ offsets[i])) for i in range(stems) for j in range(grps)]
    first = lax.ppermute(left, ("stem", "grp"), pairs)
    swapped = lax.ppermute(first, "stem", [(j, j ^ 1) for j in range(stems)])
    second = lax.ppermute(first, "stem", [(j, j ^ 2) for j in range(0, stems, 2)])
    passed = lax.ppermute(second, "stem", [(j, j ^ 1) for j in range(0, stems, 2)])
    return left, first, swapped, second, passed


def on_device(stem_tensor, left_factors, right_factors, index_labels):
    stems, grps = lax.axis_size("stem"), lax.axis_size("grp")
    s, g = lax.axis_index("stem"), lax.axis_index("grp")
    branches, p_part, upper, bond = left_factors.shape
    rows, cols = p_part * grps * LOW, upper * LOW
    if (stems % 4, grps) == (0, 4):
        firsts, cross, trade = fetch(left_factors, stems, grps), g * p_part, s // 2 % 2 * p_part
    else:
        whole = lax.all_gather(left_factors, "grp", axis=1, tiled=True)
        firsts, cross, trade = (whole.transpose(0, 2, 1, 3).reshape(branches, -1, bond),), 0 * g, 0 * s
    blocks = lax.all_to_all(stem_tensor, ("stem", "grp"), split_axis=0, concat_axis=0, tiled=True)
    place = jnp.stack([s, cross, trade]).astype(jnp.int32)
    parts = make_branches(firsts, right_factors, index_labels, place, rows, cols)
    count = stem_tensor.shape[0] // (stems * grps)
    blocks = blocks.reshape(stems * grps, count, *stem_tensor.shape[1:])
    return jnp.stack([contract(blocks[:, o], parts, stems, grps) for o in range(count)])


def solution(mesh):
    placed = (P(None, "stem", "grp"), P(None, "grp", None, None), P(), P())
    return jax.shard_map(
        on_device,
        mesh=mesh,
        in_specs=placed,
        out_specs=P(("stem", "grp"), None, None),
        check_vma=False,
    )
```
